32 devices in a mesh: grp: 2 (over y), dev: 16 (over z, x, core).
Axes of the slice: x: 2, y: 2, z: 4, core: 2. Of those that a mesh axis runs over, the one named last changes fastest.
Arguments:
- spectra: float32 [256, 2, 2, 4096], P(('grp', 'dev')), may hold values from -100 to 100
- source_pick: int32 [32], P(('grp', 'dev')), may hold values from 0 to 7
- pair_remote: int32 [2, 16, 2, 2], P('grp', 'dev'), may hold values from 0 to 7
- pair_local: int32 [2, 16, 2, 2], P('grp', 'dev'), may hold values from 0 to 7
- pair_count: int32 [2, 16, 2], P('grp', 'dev'), may hold values from 0 to 2, as said below
Outputs:
- group_corr: float32 [256, 16, 512], P(('grp', 'dev'))
- cross_corr: float32 [2, 16, 2, 2, 512], P('grp', 'dev')
The draws below stay inside these ranges and needn't reach their ends.
Inputs may be any that keep to these rules, and one draw needn't show every extreme that they name: `pair_count`: A block has no pairs with its own group and at most 2 with any other; in every group some block has exactly 2 with some other group.
All inputs are finite; a program needn't handle non-finite values.
Results may differ from the reference program's by a relative error of at most 0.0075.
Values may be sent and summed in bfloat16 or wider, within the bound.
A program may use at most 64 MiB of HBM per device.

```python
import math
import jax
import jax.numpy as jnp
from jax import lax

F = 4096
LAGS = 512
LAG_BLK = 128
BAND = 64
SEG = 2
CH_DEV = 8
XCAP = 2
BLOCKS = 32
CHANNELS = 256
N_GRP = 2
N_DEV = 16


def draw_spectra(key, part):
    noise_key, scale_key = jax.random.split(key, 2)
    bands = F // BAND
    noise_base = jnp.clip(jax.random.normal(noise_key, (CHANNELS, SEG, 2, F), jnp.float32), -6.0, 6.0)
    log_scale = jax.random.uniform(scale_key, (CHANNELS, SEG, 1, bands), jnp.float32, 0.0, math.log(10.0))
    band_scale = jnp.repeat(jnp.exp(log_scale), BAND, axis=3)
    return noise_base * band_scale


def draw_pair_count(key, part):
    base_key, block_key, offset_key = jax.random.split(key, 3)
    counts = jax.random.randint(base_key, (N_GRP, N_DEV, N_GRP), 0, XCAP + 1)
    full_block = jax.random.randint(block_key, (N_GRP, 1, 1), 0, N_DEV)
    offset = jax.random.randint(offset_key, (N_GRP, 1, 1), 1, N_GRP)
    own_group = jnp.arange(N_GRP, dtype=jnp.int32)[:, None, None]
    block_index = jnp.arange(N_DEV, dtype=jnp.int32)[None, :, None]
    other_group = jnp.arange(N_GRP, dtype=jnp.int32)[None, None, :]
    full_group = (own_group + offset) % N_GRP
    forced = (block_index == full_block) & (other_group == full_group)
    counts = jnp.where(forced, XCAP, counts)
    return jnp.where(other_group == own_group, 0, counts).astype(jnp.int32)


def touch_ends(drawn, stream_key, smallest, largest):
    longest = drawn.shape.index(max(drawn.shape))
    spots = []
    for shift in (0, 1):
        where = [jax.random.randint(jax.random.fold_in(stream_key, axis), (), 0, length) for axis, length in enumerate(drawn.shape)]
        where[longest] = (where[longest] + shift) % drawn.shape[longest]
        spots.append(tuple(where))
    return drawn.at[spots[0]].set(smallest).at[spots[1]].set(largest)


def setup_inputs(seed: int = 0) -> dict:
    arg_keys = jax.random.split(jax.random.key(seed), 6)
    spectra = draw_spectra(jax.random.fold_in(arg_keys[5], 71), 0)
    source_pick = touch_ends(jax.random.randint(arg_keys[1], (BLOCKS,), 0, CH_DEV), jax.random.fold_in(arg_keys[1], 1), 0, CH_DEV - 1).astype(jnp.int32)
    pair_remote = touch_ends(jax.random.randint(arg_keys[2], (N_GRP, N_DEV, N_GRP, XCAP), 0, CH_DEV), jax.random.fold_in(arg_keys[2], 1), 0, CH_DEV - 1).astype(jnp.int32)
    pair_local = touch_ends(jax.random.randint(arg_keys[3], (N_GRP, N_DEV, N_GRP, XCAP), 0, CH_DEV), jax.random.fold_in(arg_keys[3], 1), 0, CH_DEV - 1).astype(jnp.int32)
    pair_count = draw_pair_count(jax.random.fold_in(arg_keys[5], 71), 0)
    return {"spectra": spectra, "source_pick": source_pick, "pair_remote": pair_remote, "pair_local": pair_local, "pair_count": pair_count}


def whiten(spectra):
    magnitude = jnp.sqrt(spectra[:, :, 0] * spectra[:, :, 0] + spectra[:, :, 1] * spectra[:, :, 1])
    rows_here, segments, bins = magnitude.shape
    band_mean = lax.optimization_barrier(jnp.mean(magnitude.reshape(rows_here, segments, bins // BAND, BAND), axis=3)) + 1e-05
    divisor = jnp.repeat(band_mean, BAND, axis=2)
    return (spectra / divisor[:, :, None, :]).astype(jnp.bfloat16)

def lag_tables():
    frequency = jnp.arange(F, dtype=jnp.int32)
    lag_index = jnp.arange(LAG_BLK, dtype=jnp.int32)
    phase_index = frequency[:, None] * lag_index[None, :] % (2 * F)
    angles = phase_index.astype(jnp.float32) * (math.pi / F)
    return (jnp.cos(angles).astype(jnp.bfloat16), (-jnp.sin(angles)).astype(jnp.bfloat16))

def lag_turn(block_index):
    frequency = jnp.arange(F, dtype=jnp.int32)
    phase_index = frequency * (LAG_BLK * block_index - LAGS // 2) % (2 * F)
    angles = phase_index.astype(jnp.float32) * (math.pi / F)
    return (jnp.cos(angles), jnp.sin(angles))

def cross_to_lags(cross_real, cross_imag, tables):
    cos_table, sin_table = tables
    lag_blocks = []
    for block_index in range(LAGS // LAG_BLK):
        turn_cos, turn_sin = lag_turn(block_index)
        rot_real = (cross_real * turn_cos - cross_imag * turn_sin).astype(jnp.bfloat16)
        rot_imag = (cross_real * turn_sin + cross_imag * turn_cos).astype(jnp.bfloat16)
        lag_blocks.append(jnp.dot(rot_real, cos_table, preferred_element_type=jnp.float32) + jnp.dot(rot_imag, sin_table, preferred_element_type=jnp.float32))
    return jnp.concatenate(lag_blocks, axis=1) * F ** (-0.5)

def outer_cross(left_rows, right_rows):
    left_float = left_rows.astype(jnp.float32)
    right_float = right_rows.astype(jnp.float32)
    segments = left_rows.shape[1]
    cross_real = jnp.zeros((left_rows.shape[0], right_rows.shape[0], F), jnp.float32)
    cross_imag = jnp.zeros((left_rows.shape[0], right_rows.shape[0], F), jnp.float32)
    for segment in range(segments):
        left_real = left_float[:, segment, 0][:, None]
        left_imag = left_float[:, segment, 1][:, None]
        right_real = right_float[:, segment, 0][None]
        right_imag = right_float[:, segment, 1][None]
        cross_real = cross_real + (left_real * right_real + left_imag * right_imag)
        cross_imag = cross_imag + (left_imag * right_real - left_real * right_imag)
    inverse = 1.0 / segments
    return ((cross_real * inverse).reshape(-1, F), (cross_imag * inverse).reshape(-1, F))

def pair_cross(left_rows, right_rows):
    left_float = left_rows.astype(jnp.float32)
    right_float = right_rows.astype(jnp.float32)
    segments = left_rows.shape[1]
    cross_real = jnp.zeros((left_rows.shape[0], F), jnp.float32)
    cross_imag = jnp.zeros((left_rows.shape[0], F), jnp.float32)
    for segment in range(segments):
        left_real = left_float[:, segment, 0]
        left_imag = left_float[:, segment, 1]
        right_real = right_float[:, segment, 0]
        right_imag = right_float[:, segment, 1]
        cross_real = cross_real + (left_real * right_real + left_imag * right_imag)
        cross_imag = cross_imag + (left_imag * right_real - left_real * right_imag)
    inverse = 1.0 / segments
    return (cross_real * inverse, cross_imag * inverse)

def outer_lags(left_rows, right_rows, tables):
    cross_real, cross_imag = outer_cross(left_rows, right_rows)
    return cross_to_lags(cross_real, cross_imag, tables).reshape(left_rows.shape[0], right_rows.shape[0], LAGS)

def reference(spectra, source_pick, pair_remote, pair_local, pair_count):
    white = whiten(spectra)
    tables = lag_tables()
    blocks = white.reshape(N_GRP, N_DEV, CH_DEV, SEG, 2, F)
    sources = blocks[jnp.arange(N_GRP)[:, None], jnp.arange(N_DEV)[None, :], source_pick.reshape(N_GRP, N_DEV)]
    group_ids = jnp.repeat(jnp.arange(N_GRP, dtype=jnp.int32), N_DEV)
    dev_ids = jnp.tile(jnp.arange(N_DEV, dtype=jnp.int32), N_GRP)

    def one_block(entry):
        group_id, dev_id = entry
        return outer_lags(blocks[group_id, dev_id], sources[group_id], tables)
    group_corr = lax.map(one_block, (group_ids, dev_ids)).reshape(CHANNELS, N_DEV, LAGS)

    def one_receiver(entry):
        group_id, dev_id, remote_ids, local_ids, counts = entry
        column = blocks[:, dev_id]
        remote_rows = column[jnp.arange(N_GRP)[:, None], remote_ids]
        local_rows = blocks[group_id, dev_id][local_ids]
        cross_real, cross_imag = pair_cross(local_rows.reshape(-1, SEG, 2, F), remote_rows.reshape(-1, SEG, 2, F))
        lags_out = cross_to_lags(cross_real, cross_imag, tables).reshape(N_GRP, XCAP, LAGS)
        valid_mask = (jnp.arange(XCAP)[None, :] < counts[:, None]).astype(jnp.float32)
        return lags_out * valid_mask[:, :, None]
    cross_corr = lax.map(one_receiver, (group_ids, dev_ids, pair_remote.reshape(BLOCKS, N_GRP, XCAP), pair_local.reshape(BLOCKS, N_GRP, XCAP), pair_count.reshape(BLOCKS, N_GRP)))
    return (group_corr, cross_corr.reshape(N_GRP, N_DEV, N_GRP, XCAP, LAGS))
```

```python
import functools

import jax
import jax.numpy as jnp
import numpy as np
from jax import lax
from jax.experimental import pallas as pl
from jax.experimental.pallas import tpu as pltpu
from jax.sharding import PartitionSpec as P

MESH = pl.DeviceIdType.MESH
F = 4096
LAGS = 512
LAG_BLK = 128
BAND = 64
FINE = 64
CHUNKS = 4
WIDE = F // CHUNKS
LANES = 128


def phase_tables():
    a = np.arange(F // FINE)[:, None] * np.arange(LAG_BLK)[None, :]
    coarse = np.pi * (a * FINE % (2 * F)) / F
    b = np.arange(FINE)[:, None] * (np.arange(LAGS) - LAGS // 2)[None, :]
    fine = np.pi * (b % (2 * F)) / F
    return (
        np.stack([np.cos(coarse), np.sin(coarse)]).astype(np.float32),
        np.stack([np.cos(fine), np.sin(fine)]).astype(np.float32),
    )


def kernel(
    groups, n_dev, slots, channels, pair_rows,
    pick_ref, remote_ref, local_ref, count_ref, x_hbm, coarse_ref, fine_ref,
    group_out, cross_out,
    white, mag, gathered, row_scratch, src_f32, cos_t, sin_t, xr, xi, pr, pi, acc,
    req_out, req_in, rows_out, rows_in,
    load_sem, send_sem, recv_sem, req_send, req_recv, row_send, row_recv,
):
    g = lax.axis_index("grp")
    d = lax.axis_index("dev")
    rows = n_dev // 4
    r, c, k = d // 4, (d // 2) % 2, d % 2
    flip_c = r * 4 + (1 - c) * 2 + k
    flip_k = r * 4 + c * 2 + (1 - k)

    def row_of(t):
        return lax.rem(r + t, rows)

    def group_of(t):
        return lax.rem(g + t, groups)

    loads = []
    for s in range(2):
        for p in range(2):
            copy = pltpu.make_async_copy(x_hbm.at[:, s, p, :], white.at[s * 2 + p], load_sem.at[s * 2 + p])
            copy.start()
            loads.append(copy)

    barrier = pltpu.get_barrier_semaphore()
    for t in range(1, rows):
        pl.semaphore_signal(barrier, inc=1, device_id=(g, row_of(t) * 4 + c * 2 + k), device_id_type=MESH)
    pl.semaphore_signal(barrier, inc=1, device_id=(g, flip_c), device_id_type=MESH)
    pl.semaphore_signal(barrier, inc=1, device_id=(g, flip_k), device_id_type=MESH)
    for t in range(1, groups):
        pl.semaphore_signal(barrier, inc=1, device_id=(group_of(t), d), device_id_type=MESH)

    for t in range(1, groups):
        h = group_of(t)
        for slot in range(slots):
            req_out[t, slot:slot + 1, :] = jnp.full((1, LANES), remote_ref[0, 0, h, slot], jnp.int32)

    pl.semaphore_wait(barrier, rows + 1 + groups - 1)

    started = []

    def remote(src, dst, send, recv, target):
        return pltpu.make_async_remote_copy(
            src_ref=src, dst_ref=dst, send_sem=send, recv_sem=recv, device_id=target, device_id_type=MESH
        )

    for t in range(1, groups):
        copy = remote(req_out.at[t], req_in.at[g], req_send.at[t], req_recv.at[g], (group_of(t), d))
        copy.start()
        started.append(copy)

    for copy in loads:
        copy.wait()

    lane_i = lax.broadcasted_iota(jnp.int32, (LANES, LANES), 0)
    lane_j = lax.broadcasted_iota(jnp.int32, (LANES, LANES), 1)
    averaging = jnp.where(lane_i // BAND == lane_j // BAND, 1.0 / BAND, 0.0).astype(jnp.bfloat16)
    for s in range(2):
        for l in range(F // LANES):
            cols = slice(l * LANES, (l + 1) * LANES)
            re, im = white[2 * s, :, cols], white[2 * s + 1, :, cols]
            mag[l * channels:(l + 1) * channels, :] = jnp.sqrt(re * re + im * im)
        value = mag[...]
        high = value.astype(jnp.bfloat16)
        rest = value - high.astype(jnp.float32)
        mid = rest.astype(jnp.bfloat16)
        low = (rest - mid.astype(jnp.float32)).astype(jnp.bfloat16)
        mean = (
            jnp.dot(high, averaging, preferred_element_type=jnp.float32)
            + jnp.dot(mid, averaging, preferred_element_type=jnp.float32)
            + jnp.dot(low, averaging, preferred_element_type=jnp.float32)
        )
        mag[...] = 1.0 / (mean + 1e-05)
        for l in range(F // LANES):
            cols = slice(l * LANES, (l + 1) * LANES)
            inverse = mag[l * channels:(l + 1) * channels, :]
            for p in range(2):
                scaled = white[2 * s + p, :, cols] * inverse
                white[2 * s + p, :, cols] = scaled.astype(jnp.bfloat16).astype(jnp.float32)

    def pick_row(channel):
        for sp in range(4):
            for q in range(CHUNKS):
                row_scratch[sp * CHUNKS + q:sp * CHUNKS + q + 1, :] = white[
                    sp, pl.ds(channel, 1), q * WIDE:(q + 1) * WIDE
                ]

    pick_row(pick_ref[0])
    gathered[d] = row_scratch[...].astype(jnp.bfloat16)

    n_sent = [0]

    def forward(j, target):
        copy = remote(gathered.at[j], gathered.at[j], send_sem.at[n_sent[0]], recv_sem.at[j], (g, target))
        n_sent[0] += 1
        copy.start()
        started.append(copy)

    def arrived(j):
        remote(gathered.at[j], gathered.at[j], send_sem.at[0], recv_sem.at[j], (g, flip_k)).wait_recv()

    for t in range(1, rows):
        forward(d, row_of(t) * 4 + c * 2 + k)
    forward(d, flip_c)
    forward(d, flip_k)

    channel_id = lax.broadcasted_iota(jnp.int32, (channels, LANES), 0)
    for t in range(1, groups):
        h = group_of(t)
        remote(req_out.at[t], req_in.at[h], req_send.at[t], req_recv.at[h], (h, d)).wait_recv()
        asked = req_in[h]
        for slot in range(slots):
            chosen = channel_id == jnp.broadcast_to(asked[slot:slot + 1, :], (channels, LANES))
            chosen = jnp.concatenate([chosen] * (WIDE // LANES), axis=1)
            for sp in range(4):
                for q in range(CHUNKS):
                    part = jnp.where(chosen, white[sp, :, q * WIDE:(q + 1) * WIDE], 0.0)
                    row_scratch[sp * CHUNKS + q:sp * CHUNKS + q + 1, :] = jnp.sum(part, axis=0, keepdims=True)
            rows_out[t, slot * 16:(slot + 1) * 16, :] = row_scratch[...].astype(jnp.bfloat16)
        copy = remote(rows_out.at[t], rows_in.at[g], row_send.at[t], row_recv.at[g], (h, d))
        copy.start()
        started.append(copy)

    coarse_rows = F // FINE

    def table_part(first, last):
        @pl.loop(first, last)
        def _(a):
            ac, asin = coarse_ref[0, pl.ds(a, 1), :], coarse_ref[1, pl.ds(a, 1), :]
            here = pl.ds(pl.multiple_of(a * FINE, FINE), FINE)
            for l in range(LAGS // LANES):
                cols = slice(l * LANES, (l + 1) * LANES)
                bc, bs = fine_ref[0, :, cols], fine_ref[1, :, cols]
                cos_t[here, cols] = (ac * bc - asin * bs).astype(jnp.bfloat16)
                sin_t[here, cols] = (-(asin * bc + ac * bs)).astype(jnp.bfloat16)

    for t in range(rows):
        table_part(coarse_rows * t // rows, coarse_rows * (t + 1) // rows)
        if t > 0:
            j = row_of(t) * 4 + c * 2 + k
            arrived(j)
            forward(j, flip_c)
            forward(j, flip_k)
            j = row_of(t - 1) * 4 + (1 - c) * 2 + k
            arrived(j)
            forward(j, flip_k)
    j = row_of(rows - 1) * 4 + (1 - c) * 2 + k
    arrived(j)
    forward(j, flip_k)

    def cross_chip(first):
        for half in range(2):
            src_f32[half] = gathered[first + half].astype(jnp.float32)
        base = pl.multiple_of(first * channels, 2 * channels)

        for q in range(CHUNKS):
            for l in range(WIDE // LANES):
                cols = slice(q * WIDE + l * LANES, q * WIDE + (l + 1) * LANES)
                lanes = slice(l * LANES, (l + 1) * LANES)
                w = [white[sp, :, cols] for sp in range(4)]
                real, imag = [], []
                for half in range(2):
                    v = [
                        jnp.broadcast_to(
                            src_f32[half, sp * CHUNKS + q:sp * CHUNKS + q + 1, lanes], (channels, LANES)
                        )
                        for sp in range(4)
                    ]
                    real.append(w[0] * v[0] + w[1] * v[1] + w[2] * v[2] + w[3] * v[3])
                    imag.append(w[1] * v[0] - w[0] * v[1] + w[3] * v[2] - w[2] * v[3])
                xr[pl.ds(base, 2 * channels), cols] = jnp.concatenate(real, axis=0).astype(jnp.bfloat16)
                xi[pl.ds(base, 2 * channels), cols] = jnp.concatenate(imag, axis=0).astype(jnp.bfloat16)

    @pl.loop(0, rows)
    def _(t):
        arrived(row_of(t) * 4 + c * 2 + (1 - k))
        cross_chip(row_of(t) * 4 + c * 2)
        arrived(row_of(t) * 4 + (1 - c) * 2 + (1 - k))
        cross_chip(row_of(t) * 4 + (1 - c) * 2)

    if pair_rows:
        pr[...] = jnp.zeros_like(pr)
        pi[...] = jnp.zeros_like(pi)
    for t in range(1, groups):
        h = group_of(t)
        remote(rows_out.at[t], rows_in.at[h], row_send.at[t], row_recv.at[h], (h, d)).wait_recv()
        for slot in range(slots):
            pick_row(local_ref[0, 0, h, slot])
            there = rows_in[h, slot * 16:(slot + 1) * 16, :].astype(jnp.float32)
            here = row_scratch[...]
            w = [here[sp * CHUNKS:(sp + 1) * CHUNKS] for sp in range(4)]
            v = [there[sp * CHUNKS:(sp + 1) * CHUNKS] for sp in range(4)]
            real = w[0] * v[0] + w[1] * v[1] + w[2] * v[2] + w[3] * v[3]
            imag = w[1] * v[0] - w[0] * v[1] + w[3] * v[2] - w[2] * v[3]
            row = (t - 1) * slots + slot
            for q in range(CHUNKS):
                pr[row:row + 1, q * WIDE:(q + 1) * WIDE] = real[q:q + 1]
                pi[row:row + 1, q * WIDE:(q + 1) * WIDE] = imag[q:q + 1]
    if pair_rows:
        xr[n_dev * channels:, :] = pr[...].astype(jnp.bfloat16)
        xi[n_dev * channels:, :] = pi[...].astype(jnp.bfloat16)

    acc[...] = jnp.zeros_like(acc)
    depth = 1024

    @pl.loop(0, F // depth)
    def _(step):
        here = pl.ds(pl.multiple_of(step * depth, depth), depth)
        acc[...] += jnp.dot(xr[:, here], cos_t[here, :], preferred_element_type=jnp.float32) + jnp.dot(
            xi[:, here], sin_t[here, :], preferred_element_type=jnp.float32
        )

    scale = 0.5 * F ** (-0.5)
    group_out[...] = acc[:n_dev * channels, :].reshape(n_dev, channels, LAGS) * scale
    cross_out[g] = jnp.zeros((slots, LAGS), jnp.float32)
    for t in range(1, groups):
        h = group_of(t)
        for slot in range(slots):
            row = n_dev * channels + (t - 1) * slots + slot
            valid = jnp.where(slot < count_ref[0, 0, h], scale, 0.0)
            cross_out[h, slot:slot + 1, :] = acc[row:row + 1, :] * valid

    for copy in started:
        copy.wait_send()


def solution(mesh):
    groups, n_dev = mesh.shape["grp"], mesh.shape["dev"]
    coarse, fine = phase_tables()

    def on_device(spectra, source_pick, pair_remote, pair_local, pair_count):
        channels = spectra.shape[0]
        slots = pair_remote.shape[3]
        pair_rows = -(-((groups - 1) * slots) // 16) * 16
        total = n_dev * channels + pair_rows
        smem = pl.BlockSpec(memory_space=pltpu.SMEM)
        vmem = pl.BlockSpec(memory_space=pltpu.VMEM)
        f32, bf16 = jnp.float32, jnp.bfloat16
        group_corr, cross_corr = pl.pallas_call(
            functools.partial(kernel, groups, n_dev, slots, channels, pair_rows),
            out_shape=(
                jax.ShapeDtypeStruct((n_dev, channels, LAGS), f32),
                jax.ShapeDtypeStruct((groups, slots, LAGS), f32),
            ),
            in_specs=[smem, smem, smem, smem, pl.BlockSpec(memory_space=pl.ANY), vmem, vmem],
            out_specs=(vmem, vmem),
            scratch_shapes=[
                pltpu.VMEM((4, channels, F), f32),
                pltpu.VMEM((F // LANES * channels, LANES), f32),
                pltpu.VMEM((n_dev, 16, WIDE), bf16),
                pltpu.VMEM((16, WIDE), f32),
                pltpu.VMEM((2, 16, WIDE), f32),
                pltpu.VMEM((F, LAGS), bf16),
                pltpu.VMEM((F, LAGS), bf16),
                pltpu.VMEM((total, F), bf16),
                pltpu.VMEM((total, F), bf16),
                pltpu.VMEM((16, F), f32),
                pltpu.VMEM((16, F), f32),
                pltpu.VMEM((total, LAGS), f32),
                pltpu.VMEM((groups, 8, LANES), jnp.int32),
                pltpu.VMEM((groups, 8, LANES), jnp.int32),
                pltpu.VMEM((groups, slots * 16, WIDE), bf16),
                pltpu.VMEM((groups, slots * 16, WIDE), bf16),
                pltpu.SemaphoreType.DMA((4,)),
                pltpu.SemaphoreType.DMA((n_dev,)),
                pltpu.SemaphoreType.DMA((n_dev,)),
                pltpu.SemaphoreType.DMA((groups,)),
                pltpu.SemaphoreType.DMA((groups,)),
                pltpu.SemaphoreType.DMA((groups,)),
                pltpu.SemaphoreType.DMA((groups,)),
            ],
            compiler_params=pltpu.CompilerParams(
                collective_id=0, has_side_effects=True, vmem_limit_bytes=56 << 20
            ),
        )(source_pick, pair_remote, pair_local, pair_count, spectra, jnp.asarray(coarse), jnp.asarray(fine))
        return (
            jnp.transpose(group_corr, (1, 0, 2)),
            cross_corr.reshape(1, 1, groups, slots, LAGS),
        )

    return jax.shard_map(
        on_device,
        mesh=mesh,
        in_specs=(
            P(("grp", "dev"), None, None, None),
            P(("grp", "dev")),
            P("grp", "dev", None, None),
            P("grp", "dev", None, None),
            P("grp", "dev", None),
        ),
        out_specs=(P(("grp", "dev"), None, None), P("grp", "dev", None, None, None)),
        check_vma=False,
    )
```

```python
import functools

import jax
import jax.numpy as jnp
import numpy as np
from jax import lax
from jax.experimental import pallas as pl
from jax.experimental.pallas import tpu as pltpu
from jax.sharding import PartitionSpec as P

MESH = pl.DeviceIdType.MESH
F = 4096
LAGS = 512
LAG_BLK = 128
BAND = 64
FINE = 64
CHUNKS = 4
WIDE = F // CHUNKS
LANES = 128
PARTS = 2
PART = F // PARTS


def phase_tables():
    a = np.arange(F // FINE)[:, None] * np.arange(LAG_BLK)[None, :]
    coarse = np.pi * (a * FINE % (2 * F)) / F
    b = np.arange(FINE)[:, None] * (np.arange(LAGS) - LAGS // 2)[None, :]
    fine = np.pi * (b % (2 * F)) / F
    return (
        np.stack([np.cos(coarse), np.sin(coarse)]).astype(np.float32),
        np.stack([np.cos(fine), np.sin(fine)]).astype(np.float32),
    )


def kernel(
    groups, n_dev, slots, channels, pair_rows,
    pick_ref, remote_ref, local_ref, count_ref, x_hbm, coarse_hbm, fine_hbm,
    group_out, cross_out,
    raw, white, mag, gathered, row_scratch, src_f32, cos_t, sin_t, xr, xi, pr, pi, acc,
    req_out, req_in, rows_out, rows_in,
    coarse_ref, fine_ref, load_sem, table_sem, send_sem, recv_sem, req_send, req_recv, row_send, row_recv,
):
    g = lax.axis_index("grp")
    d = lax.axis_index("dev")
    rows = n_dev // 4
    r, c, k = d // 4, (d // 2) % 2, d % 2
    flip_c = r * 4 + (1 - c) * 2 + k
    flip_k = r * 4 + c * 2 + (1 - k)

    def row_of(t):
        return lax.rem(r + t, rows)

    def group_of(t):
        return lax.rem(g + t, groups)

    loads = []
    for q in range(PARTS):
        cols = pl.ds(q * PART, PART)
        for sp in range(4):
            loads.append(pltpu.make_async_copy(
                x_hbm.at[:, sp // 2, sp % 2, cols], raw.at[sp, :, cols], load_sem.at[q * 4 + sp]
            ))
            loads[-1].start()
    table_loads = [
        pltpu.make_async_copy(coarse_hbm, coarse_ref, table_sem.at[0]),
        pltpu.make_async_copy(fine_hbm, fine_ref, table_sem.at[1]),
    ]
    for copy in table_loads:
        copy.start()

    barrier = pltpu.get_barrier_semaphore()
    for t in range(1, rows):
        pl.semaphore_signal(barrier, inc=1, device_id=(g, row_of(t) * 4 + c * 2 + k), device_id_type=MESH)
    pl.semaphore_signal(barrier, inc=1, device_id=(g, flip_c), device_id_type=MESH)
    pl.semaphore_signal(barrier, inc=1, device_id=(g, flip_k), device_id_type=MESH)
    for t in range(1, groups):
        pl.semaphore_signal(barrier, inc=1, device_id=(group_of(t), d), device_id_type=MESH)

    for t in range(1, groups):
        h = group_of(t)
        for slot in range(slots):
            req_out[t, slot:slot + 1, :] = jnp.full((1, LANES), remote_ref[0, 0, h, slot], jnp.int32)

    started = []

    def remote(src, dst, send, recv, target):
        return pltpu.make_async_remote_copy(
            src_ref=src, dst_ref=dst, send_sem=send, recv_sem=recv, device_id=target, device_id_type=MESH
        )

    lane_i = lax.broadcasted_iota(jnp.int32, (LANES, LANES), 0)
    lane_j = lax.broadcasted_iota(jnp.int32, (LANES, LANES), 1)
    averaging = jnp.where(lane_i // BAND == lane_j // BAND, 1.0 / BAND, 0.0).astype(jnp.bfloat16)
    width = PART // CHUNKS

    def whiten(q):
        for copy in loads[q * 4:(q + 1) * 4]:
            copy.wait()
        tiles = PART // LANES
        for s in range(2):
            for l in range(tiles):
                cols = slice(q * PART + l * LANES, q * PART + (l + 1) * LANES)
                re, im = raw[2 * s, :, cols], raw[2 * s + 1, :, cols]
                mag[(s * tiles + l) * channels:(s * tiles + l + 1) * channels, :] = jnp.sqrt(re * re + im * im)
        value = mag[...]
        high = value.astype(jnp.bfloat16)
        rest = value - high.astype(jnp.float32)
        mid = rest.astype(jnp.bfloat16)
        low = (rest - mid.astype(jnp.float32)).astype(jnp.bfloat16)
        mean = (
            jnp.dot(high, averaging, preferred_element_type=jnp.float32)
            + jnp.dot(mid, averaging, preferred_element_type=jnp.float32)
            + jnp.dot(low, averaging, preferred_element_type=jnp.float32)
        )
        mag[...] = 1.0 / (mean + 1e-05)
        for s in range(2):
            for l in range(tiles):
                cols = slice(q * PART + l * LANES, q * PART + (l + 1) * LANES)
                inverse = mag[(s * tiles + l) * channels:(s * tiles + l + 1) * channels, :]
                for p in range(2):
                    scaled = raw[2 * s + p, :, cols] * inverse
                    white[2 * s + p, :, cols] = scaled.astype(jnp.bfloat16).astype(jnp.float32)

    def pick_row(channel):
        for sp in range(4):
            for i in range(CHUNKS):
                row_scratch[sp * CHUNKS + i:sp * CHUNKS + i + 1, :] = white[
                    sp, pl.ds(channel, 1), i * WIDE:(i + 1) * WIDE
                ]

    def pick_source(q):
        for sp in range(4):
            for i in range(CHUNKS):
                first = q * PART + i * width
                row_scratch[sp * CHUNKS + i:sp * CHUNKS + i + 1, :width] = white[
                    sp, pl.ds(pick_ref[0], 1), first:first + width
                ]
        gathered[q, d] = row_scratch[:, :width].astype(jnp.bfloat16)

    n_sent = [0]

    def forward(q, j, target):
        copy = remote(
            gathered.at[q, j], gathered.at[q, j], send_sem.at[n_sent[0]], recv_sem.at[q, j], (g, target)
        )
        n_sent[0] += 1
        copy.start()
        started.append(copy)

    def arrived(q, j):
        remote(gathered.at[q, j], gathered.at[q, j], send_sem.at[0], recv_sem.at[q, j], (g, flip_k)).wait_recv()

    def send_own(q):
        for t in range(1, rows):
            forward(q, d, row_of(t) * 4 + c * 2 + k)
        forward(q, d, flip_c)
        forward(q, d, flip_k)

    def pass_column(q):
        for t in range(1, rows):
            j = row_of(t) * 4 + c * 2 + k
            arrived(q, j)
            forward(q, j, flip_c)
            forward(q, j, flip_k)

    def pass_other(q):
        for t in range(rows):
            j = row_of(t) * 4 + (1 - c) * 2 + k
            arrived(q, j)
            forward(q, j, flip_k)

    whiten(0)
    pick_source(0)
    pl.semaphore_wait(barrier, rows + 1 + groups - 1)
    send_own(0)
    for t in range(1, groups):
        copy = remote(req_out.at[t], req_in.at[g], req_send.at[t], req_recv.at[g], (group_of(t), d))
        copy.start()
        started.append(copy)
    for q in range(1, PARTS):
        whiten(q)
        pick_source(q)
        send_own(q)

    channel_id = lax.broadcasted_iota(jnp.int32, (channels, LANES), 0)
    for t in range(1, groups):
        h = group_of(t)
        remote(req_out.at[t], req_in.at[h], req_send.at[t], req_recv.at[h], (h, d)).wait_recv()
        asked = req_in[h]
        for slot in range(slots):
            chosen = channel_id == jnp.broadcast_to(asked[slot:slot + 1, :], (channels, LANES))
            chosen = jnp.concatenate([chosen] * (WIDE // LANES), axis=1)
            for sp in range(4):
                for q in range(CHUNKS):
                    part = jnp.where(chosen, white[sp, :, q * WIDE:(q + 1) * WIDE], 0.0)
                    row_scratch[sp * CHUNKS + q:sp * CHUNKS + q + 1, :] = jnp.sum(part, axis=0, keepdims=True)
            rows_out[t, slot * 16:(slot + 1) * 16, :] = row_scratch[...].astype(jnp.bfloat16)
        copy = remote(rows_out.at[t], rows_in.at[g], row_send.at[t], row_recv.at[g], (h, d))
        copy.start()
        started.append(copy)

    for copy in table_loads:
        copy.wait()
    coarse_rows = F // FINE

    def table_part(first, last):
        @pl.loop(first, last)
        def _(a):
            ac, asin = coarse_ref[0, pl.ds(a, 1), :], coarse_ref[1, pl.ds(a, 1), :]
            here = pl.ds(pl.multiple_of(a * FINE, FINE), FINE)
            for l in range(LAGS // LANES):
                cols = slice(l * LANES, (l + 1) * LANES)
                bc, bs = fine_ref[0, :, cols], fine_ref[1, :, cols]
                cos_t[here, cols] = (ac * bc - asin * bs).astype(jnp.bfloat16)
                sin_t[here, cols] = (-(asin * bc + ac * bs)).astype(jnp.bfloat16)

    def cross_chip(q, first):
        for half in range(2):
            src_f32[half] = gathered[q, first + half].astype(jnp.float32)
        base = pl.multiple_of(first * channels, 2 * channels)
        for i in range(CHUNKS):
            for l in range(width // LANES):
                start = q * PART + i * width + l * LANES
                cols = slice(start, start + LANES)
                lanes = slice(l * LANES, (l + 1) * LANES)
                w = [white[sp, :, cols] for sp in range(4)]
                real, imag = [], []
                for half in range(2):
                    v = [
                        jnp.broadcast_to(
                            src_f32[half, sp * CHUNKS + i:sp * CHUNKS + i + 1, lanes], (channels, LANES)
                        )
                        for sp in range(4)
                    ]
                    real.append(w[0] * v[0] + w[1] * v[1] + w[2] * v[2] + w[3] * v[3])
                    imag.append(w[1] * v[0] - w[0] * v[1] + w[3] * v[2] - w[2] * v[3])
                xr[pl.ds(base, 2 * channels), cols] = jnp.concatenate(real, axis=0).astype(jnp.bfloat16)
                xi[pl.ds(base, 2 * channels), cols] = jnp.concatenate(imag, axis=0).astype(jnp.bfloat16)

    def cross_part(q):
        @pl.loop(0, rows)
        def _(t):
            arrived(q, row_of(t) * 4 + c * 2 + (1 - k))
            cross_chip(q, row_of(t) * 4 + c * 2)

        @pl.loop(0, rows)
        def _(t):
            arrived(q, row_of(t) * 4 + (1 - c) * 2 + (1 - k))
            cross_chip(q, row_of(t) * 4 + (1 - c) * 2)

    def multiply(q):
        here = slice(q * PART, (q + 1) * PART)
        part = jnp.dot(xr[:, here], cos_t[here, :], preferred_element_type=jnp.float32) + jnp.dot(
            xi[:, here], sin_t[here, :], preferred_element_type=jnp.float32
        )
        acc[...] = part if q == 0 else acc[...] + part

    table_part(0, coarse_rows // 2)
    pass_column(0)
    table_part(coarse_rows // 2, coarse_rows)
    for q in range(1, PARTS):
        pass_column(q)
        pass_other(q - 1)

    if pair_rows:
        pr[...] = jnp.zeros_like(pr)
        pi[...] = jnp.zeros_like(pi)
    for t in range(1, groups):
        h = group_of(t)
        remote(rows_out.at[t], rows_in.at[h], row_send.at[t], row_recv.at[h], (h, d)).wait_recv()
        for slot in range(slots):
            pick_row(local_ref[0, 0, h, slot])
            there = rows_in[h, slot * 16:(slot + 1) * 16, :].astype(jnp.float32)
            here = row_scratch[...]
            w = [here[sp * CHUNKS:(sp + 1) * CHUNKS] for sp in range(4)]
            v = [there[sp * CHUNKS:(sp + 1) * CHUNKS] for sp in range(4)]
            real = w[0] * v[0] + w[1] * v[1] + w[2] * v[2] + w[3] * v[3]
            imag = w[1] * v[0] - w[0] * v[1] + w[3] * v[2] - w[2] * v[3]
            row = (t - 1) * slots + slot
            for q in range(CHUNKS):
                pr[row:row + 1, q * WIDE:(q + 1) * WIDE] = real[q:q + 1]
                pi[row:row + 1, q * WIDE:(q + 1) * WIDE] = imag[q:q + 1]
    if pair_rows:
        xr[n_dev * channels:, :] = pr[...].astype(jnp.bfloat16)
        xi[n_dev * channels:, :] = pi[...].astype(jnp.bfloat16)

    for q in range(PARTS):
        cross_part(q)
        if q + 1 < PARTS:
            pass_other(PARTS - 1)
        multiply(q)

    scale = 0.5 * F ** (-0.5)
    for j in range(n_dev):
        group_out[:, j, :] = acc[j * channels:(j + 1) * channels, :] * scale
    cross_out[g] = jnp.zeros((slots, LAGS), jnp.float32)
    for t in range(1, groups):
        h = group_of(t)
        for slot in range(slots):
            row = n_dev * channels + (t - 1) * slots + slot
            valid = jnp.where(slot < count_ref[0, 0, h], scale, 0.0)
            cross_out[h, slot:slot + 1, :] = acc[row:row + 1, :] * valid

    for copy in started:
        copy.wait_send()


def solution(mesh):
    groups, n_dev = mesh.shape["grp"], mesh.shape["dev"]
    coarse, fine = phase_tables()

    def on_device(spectra, source_pick, pair_remote, pair_local, pair_count):
        channels = spectra.shape[0]
        slots = pair_remote.shape[3]
        pair_rows = -(-((groups - 1) * slots) // 16) * 16
        total = n_dev * channels + pair_rows
        smem = pl.BlockSpec(memory_space=pltpu.SMEM)
        hbm = pl.BlockSpec(memory_space=pl.ANY)
        vmem = pl.BlockSpec(memory_space=pltpu.VMEM)
        f32, bf16 = jnp.float32, jnp.bfloat16
        group_corr, cross_corr = pl.pallas_call(
            functools.partial(kernel, groups, n_dev, slots, channels, pair_rows),
            out_shape=(
                jax.ShapeDtypeStruct((channels, n_dev, LAGS), f32),
                jax.ShapeDtypeStruct((groups, slots, LAGS), f32),
            ),
            in_specs=[smem, smem, smem, smem, hbm, hbm, hbm],
            out_specs=(vmem, vmem),
            scratch_shapes=[
                pltpu.VMEM((4, channels, F), f32),
                pltpu.VMEM((4, channels, F), f32),
                pltpu.VMEM((2 * PART // LANES * channels, LANES), f32),
                pltpu.VMEM((PARTS, n_dev, 16, PART // CHUNKS), bf16),
                pltpu.VMEM((16, WIDE), f32),
                pltpu.VMEM((2, 16, PART // CHUNKS), f32),
                pltpu.VMEM((F, LAGS), bf16),
                pltpu.VMEM((F, LAGS), bf16),
                pltpu.VMEM((total, F), bf16),
                pltpu.VMEM((total, F), bf16),
                pltpu.VMEM((16, F), f32),
                pltpu.VMEM((16, F), f32),
                pltpu.VMEM((total, LAGS), f32),
                pltpu.VMEM((groups, 8, LANES), jnp.int32),
                pltpu.VMEM((groups, 8, LANES), jnp.int32),
                pltpu.VMEM((groups, slots * 16, WIDE), bf16),
                pltpu.VMEM((groups, slots * 16, WIDE), bf16),
                pltpu.VMEM(coarse.shape, f32),
                pltpu.VMEM(fine.shape, f32),
                pltpu.SemaphoreType.DMA((4 * PARTS,)),
                pltpu.SemaphoreType.DMA((2,)),
                pltpu.SemaphoreType.DMA((n_dev * PARTS,)),
                pltpu.SemaphoreType.DMA((PARTS, n_dev)),
                pltpu.SemaphoreType.DMA((groups,)),
                pltpu.SemaphoreType.DMA((groups,)),
                pltpu.SemaphoreType.DMA((groups,)),
                pltpu.SemaphoreType.DMA((groups,)),
            ],
            compiler_params=pltpu.CompilerParams(
                collective_id=0, has_side_effects=True, vmem_limit_bytes=56 << 20
            ),
        )(source_pick, pair_remote, pair_local, pair_count, spectra, jnp.asarray(coarse), jnp.asarray(fine))
        return (
            group_corr,
            cross_corr.reshape(1, 1, groups, slots, LAGS),
        )

    return jax.shard_map(
        on_device,
        mesh=mesh,
        in_specs=(
            P(("grp", "dev"), None, None, None),
            P(("grp", "dev")),
            P("grp", "dev", None, None),
            P("grp", "dev", None, None),
            P("grp", "dev", None),
        ),
        out_specs=(P(("grp", "dev"), None, None), P("grp", "dev", None, None, None)),
        check_vma=False,
    )
```

```python
import functools

import jax
import jax.numpy as jnp
import numpy as np
from jax import lax
from jax.experimental import pallas as pl
from jax.experimental.pallas import tpu as pltpu
from jax.sharding import PartitionSpec as P

MESH = pl.DeviceIdType.MESH
F = 4096
LAGS = 512
LAG_BLK = 128
BAND = 64
FINE = 64
CHUNKS = 4
WIDE = F // CHUNKS
LANES = 128
PARTS = 2
TABLE_CUTS = (6, 10, 14, 16)
PART = F // PARTS


def phase_tables():
    a = np.arange(F // FINE)[:, None] * np.arange(LAG_BLK)[None, :]
    coarse = np.pi * (a * FINE % (2 * F)) / F
    b = np.arange(FINE)[:, None] * (np.arange(LAGS) - LAGS // 2)[None, :]
    fine = np.pi * (b % (2 * F)) / F
    return (
        np.stack([np.cos(coarse), np.sin(coarse)]).astype(np.float32),
        np.stack([np.cos(fine), np.sin(fine)]).astype(np.float32),
    )


def kernel(
    groups, n_dev, slots, channels, pair_rows,
    pick_ref, remote_ref, local_ref, x_hbm, coarse_hbm, fine_hbm,
    group_out, cross_out,
    raw, white, mag, gathered, row_scratch, src_f32, cos_t, sin_t, xr, xi, pr, pi, acc,
    req_out, req_in, rows_out, rows_in,
    coarse_ref, fine_ref, load_sem, table_sem, send_sem, recv_sem, req_send, req_recv, row_send, row_recv,
):
    g = lax.axis_index("grp")
    d = lax.axis_index("dev")
    rows = n_dev // 4
    r, c, k = d // 4, (d // 2) % 2, d % 2
    flip_c = r * 4 + (1 - c) * 2 + k
    flip_k = r * 4 + c * 2 + (1 - k)

    def row_of(t):
        return lax.rem(r + t, rows)

    def group_of(t):
        return lax.rem(g + t, groups)

    loads = []
    for q in range(PARTS):
        cols = pl.ds(q * PART, PART)
        for sp in range(4):
            loads.append(pltpu.make_async_copy(
                x_hbm.at[:, sp // 2, sp % 2, cols], raw.at[sp, :, cols], load_sem.at[q * 4 + sp]
            ))
            loads[-1].start()
    table_loads = [
        pltpu.make_async_copy(coarse_hbm, coarse_ref, table_sem.at[0]),
        pltpu.make_async_copy(fine_hbm, fine_ref, table_sem.at[1]),
    ]
    for copy in table_loads:
        copy.start()

    barrier = pltpu.get_barrier_semaphore()
    for t in range(1, rows):
        pl.semaphore_signal(barrier, inc=1, device_id=(g, row_of(t) * 4 + c * 2 + k), device_id_type=MESH)
    pl.semaphore_signal(barrier, inc=1, device_id=(g, flip_c), device_id_type=MESH)
    pl.semaphore_signal(barrier, inc=1, device_id=(g, flip_k), device_id_type=MESH)
    for t in range(1, groups):
        pl.semaphore_signal(barrier, inc=1, device_id=(group_of(t), d), device_id_type=MESH)

    for t in range(1, groups):
        h = group_of(t)
        for slot in range(slots):
            req_out[t, slot:slot + 1, :] = jnp.full((1, LANES), remote_ref[0, 0, h, slot], jnp.int32)

    started = []

    def remote(src, dst, send, recv, target):
        return pltpu.make_async_remote_copy(
            src_ref=src, dst_ref=dst, send_sem=send, recv_sem=recv, device_id=target, device_id_type=MESH
        )

    lane_i = lax.broadcasted_iota(jnp.int32, (LANES, LANES), 0)
    lane_j = lax.broadcasted_iota(jnp.int32, (LANES, LANES), 1)
    averaging = jnp.where(lane_i // BAND == lane_j // BAND, 1.0 / BAND, 0.0).astype(jnp.bfloat16)
    width = PART // CHUNKS

    def whiten(q):
        for copy in loads[q * 4:(q + 1) * 4]:
            copy.wait()
        tiles = PART // LANES
        for s in range(2):
            for l in range(tiles):
                cols = slice(q * PART + l * LANES, q * PART + (l + 1) * LANES)
                re, im = raw[2 * s, :, cols], raw[2 * s + 1, :, cols]
                mag[(s * tiles + l) * channels:(s * tiles + l + 1) * channels, :] = jnp.sqrt(re * re + im * im)
        value = mag[...]
        high = value.astype(jnp.bfloat16)
        rest = value - high.astype(jnp.float32)
        mid = rest.astype(jnp.bfloat16)
        low = (rest - mid.astype(jnp.float32)).astype(jnp.bfloat16)
        mean = (
            jnp.dot(high, averaging, preferred_element_type=jnp.float32)
            + jnp.dot(mid, averaging, preferred_element_type=jnp.float32)
            + jnp.dot(low, averaging, preferred_element_type=jnp.float32)
        )
        mag[...] = 1.0 / (mean + 1e-05)
        for s in range(2):
            for l in range(tiles):
                cols = slice(q * PART + l * LANES, q * PART + (l + 1) * LANES)
                inverse = mag[(s * tiles + l) * channels:(s * tiles + l + 1) * channels, :]
                for p in range(2):
                    scaled = raw[2 * s + p, :, cols] * inverse
                    white[2 * s + p, :, cols] = scaled.astype(jnp.bfloat16).astype(jnp.float32)

    def pick_row(channel):
        for sp in range(4):
            for i in range(CHUNKS):
                row_scratch[sp * CHUNKS + i:sp * CHUNKS + i + 1, :] = white[
                    sp, pl.ds(channel, 1), i * WIDE:(i + 1) * WIDE
                ]

    def pick_source(q):
        for sp in range(4):
            for i in range(CHUNKS):
                first = q * PART + i * width
                row_scratch[sp * CHUNKS + i:sp * CHUNKS + i + 1, :width] = white[
                    sp, pl.ds(pick_ref[0], 1), first:first + width
                ]
        gathered[q, d] = row_scratch[:, :width].astype(jnp.bfloat16)

    n_sent = [0]

    def forward(q, j, target):
        copy = remote(
            gathered.at[q, j], gathered.at[q, j], send_sem.at[n_sent[0]], recv_sem.at[q, j], (g, target)
        )
        n_sent[0] += 1
        copy.start()
        started.append(copy)

    def arrived(q, j):
        remote(gathered.at[q, j], gathered.at[q, j], send_sem.at[0], recv_sem.at[q, j], (g, flip_k)).wait_recv()

    def send_own(q):
        for t in range(1, rows):
            forward(q, d, row_of(t) * 4 + c * 2 + k)
        forward(q, d, flip_c)
        forward(q, d, flip_k)

    def pass_column(q):
        for t in range(1, rows):
            j = row_of(t) * 4 + c * 2 + k
            arrived(q, j)
            forward(q, j, flip_c)
            forward(q, j, flip_k)

    def pass_other(q):
        for t in range(rows):
            j = row_of(t) * 4 + (1 - c) * 2 + k
            arrived(q, j)
            forward(q, j, flip_k)

    coarse_rows = F // FINE

    cuts = [coarse_rows * n // 16 for n in TABLE_CUTS]

    def table_part(first, last):
        if first == last:
            return

        @pl.loop(first, last)
        def _(a):
            ac, asin = coarse_ref[0, pl.ds(a, 1), :], coarse_ref[1, pl.ds(a, 1), :]
            here = pl.ds(pl.multiple_of(a * FINE, FINE), FINE)
            for l in range(LAGS // LANES):
                cols = slice(l * LANES, (l + 1) * LANES)
                bc, bs = fine_ref[0, :, cols], fine_ref[1, :, cols]
                cos_t[here, cols] = (ac * bc - asin * bs).astype(jnp.bfloat16)
                sin_t[here, cols] = (-(asin * bc + ac * bs)).astype(jnp.bfloat16)

    whiten(0)
    pick_source(0)
    for copy in table_loads:
        copy.wait()
    table_part(0, cuts[0])
    pl.semaphore_wait(barrier, rows + 1 + groups - 1)
    send_own(0)
    for t in range(1, groups):
        copy = remote(req_out.at[t], req_in.at[g], req_send.at[t], req_recv.at[g], (group_of(t), d))
        copy.start()
        started.append(copy)
    for q in range(1, PARTS):
        whiten(q)
        pick_source(q)
        send_own(q)

    channel_id = lax.broadcasted_iota(jnp.int32, (channels, LANES), 0)
    for t in range(1, groups):
        h = group_of(t)
        remote(req_out.at[t], req_in.at[h], req_send.at[t], req_recv.at[h], (h, d)).wait_recv()
        asked = req_in[h]
        for slot in range(slots):
            chosen = channel_id == jnp.broadcast_to(asked[slot:slot + 1, :], (channels, LANES))
            chosen = jnp.concatenate([chosen] * (WIDE // LANES), axis=1)
            for sp in range(4):
                for q in range(CHUNKS):
                    part = jnp.where(chosen, white[sp, :, q * WIDE:(q + 1) * WIDE], 0.0)
                    row_scratch[sp * CHUNKS + q:sp * CHUNKS + q + 1, :] = jnp.sum(part, axis=0, keepdims=True)
            rows_out[t, slot * 16:(slot + 1) * 16, :] = row_scratch[...].astype(jnp.bfloat16)
        copy = remote(rows_out.at[t], rows_in.at[g], row_send.at[t], row_recv.at[g], (h, d))
        copy.start()
        started.append(copy)

    def cross_chip(q, first):
        for half in range(2):
            src_f32[half] = gathered[q, first + half].astype(jnp.float32)
        base = pl.multiple_of(first * channels, 2 * channels)
        for i in range(CHUNKS):
            for l in range(width // LANES):
                start = q * PART + i * width + l * LANES
                cols = slice(start, start + LANES)
                lanes = slice(l * LANES, (l + 1) * LANES)
                w = [white[sp, :, cols] for sp in range(4)]
                real, imag = [], []
                for half in range(2):
                    v = [
                        jnp.broadcast_to(
                            src_f32[half, sp * CHUNKS + i:sp * CHUNKS + i + 1, lanes], (channels, LANES)
                        )
                        for sp in range(4)
                    ]
                    real.append(w[0] * v[0] + w[1] * v[1] + w[2] * v[2] + w[3] * v[3])
                    imag.append(w[1] * v[0] - w[0] * v[1] + w[3] * v[2] - w[2] * v[3])
                xr[pl.ds(base, 2 * channels), cols] = jnp.concatenate(real, axis=0).astype(jnp.bfloat16)
                xi[pl.ds(base, 2 * channels), cols] = jnp.concatenate(imag, axis=0).astype(jnp.bfloat16)

    def cross_part(q):
        @pl.loop(0, rows)
        def _(t):
            arrived(q, row_of(t) * 4 + c * 2 + (1 - k))
            cross_chip(q, row_of(t) * 4 + c * 2)

        @pl.loop(0, rows)
        def _(t):
            arrived(q, row_of(t) * 4 + (1 - c) * 2 + (1 - k))
            cross_chip(q, row_of(t) * 4 + (1 - c) * 2)

    def multiply(q):
        here = slice(q * PART, (q + 1) * PART)
        part = jnp.dot(xr[:, here], cos_t[here, :], preferred_element_type=jnp.float32) + jnp.dot(
            xi[:, here], sin_t[here, :], preferred_element_type=jnp.float32
        )
        acc[...] = part if q == 0 else acc[...] + part

    table_part(cuts[0], cuts[1])
    pass_column(0)
    table_part(cuts[1], cuts[2])
    for q in range(1, PARTS):
        pass_column(q)
        table_part(cuts[2], cuts[3])
        pass_other(q - 1)
    table_part(cuts[3], coarse_rows)

    if pair_rows:
        pr[...] = jnp.zeros_like(pr)
        pi[...] = jnp.zeros_like(pi)
    for t in range(1, groups):
        h = group_of(t)
        remote(rows_out.at[t], rows_in.at[h], row_send.at[t], row_recv.at[h], (h, d)).wait_recv()
        for slot in range(slots):
            pick_row(local_ref[0, 0, h, slot])
            there = rows_in[h, slot * 16:(slot + 1) * 16, :].astype(jnp.float32)
            here = row_scratch[...]
            w = [here[sp * CHUNKS:(sp + 1) * CHUNKS] for sp in range(4)]
            v = [there[sp * CHUNKS:(sp + 1) * CHUNKS] for sp in range(4)]
            real = w[0] * v[0] + w[1] * v[1] + w[2] * v[2] + w[3] * v[3]
            imag = w[1] * v[0] - w[0] * v[1] + w[3] * v[2] - w[2] * v[3]
            row = (t - 1) * slots + slot
            for q in range(CHUNKS):
                pr[row:row + 1, q * WIDE:(q + 1) * WIDE] = real[q:q + 1]
                pi[row:row + 1, q * WIDE:(q + 1) * WIDE] = imag[q:q + 1]
    if pair_rows:
        xr[n_dev * channels:, :] = pr[...].astype(jnp.bfloat16)
        xi[n_dev * channels:, :] = pi[...].astype(jnp.bfloat16)

    for q in range(PARTS):
        cross_part(q)
        if q + 1 < PARTS:
            pass_other(PARTS - 1)
        multiply(q)

    for j in range(n_dev):
        group_out[:, j, :] = acc[j * channels:(j + 1) * channels, :]
    cross_out[g] = jnp.zeros((slots, LAGS), jnp.float32)
    for t in range(1, groups):
        row = n_dev * channels + (t - 1) * slots
        cross_out[group_of(t)] = acc[row:row + slots, :]

    for copy in started:
        copy.wait_send()


def solution(mesh):
    groups, n_dev = mesh.shape["grp"], mesh.shape["dev"]
    coarse, fine = phase_tables()

    def on_device(spectra, source_pick, pair_remote, pair_local, pair_count):
        channels = spectra.shape[0]
        slots = pair_remote.shape[3]
        pair_rows = -(-((groups - 1) * slots) // 16) * 16
        total = n_dev * channels + pair_rows
        smem = pl.BlockSpec(memory_space=pltpu.SMEM)
        hbm = pl.BlockSpec(memory_space=pltpu.HBM)
        vmem = pl.BlockSpec(memory_space=pltpu.VMEM)
        f32, bf16 = jnp.float32, jnp.bfloat16
        group_corr, cross_corr = pl.pallas_call(
            functools.partial(kernel, groups, n_dev, slots, channels, pair_rows),
            out_shape=(
                jax.ShapeDtypeStruct((channels, n_dev, LAGS), f32),
                jax.ShapeDtypeStruct((groups, slots, LAGS), f32),
            ),
            in_specs=[smem, smem, smem, hbm, hbm, hbm],
            out_specs=(vmem, vmem),
            scratch_shapes=[
                pltpu.VMEM((4, channels, F), f32),
                pltpu.VMEM((4, channels, F), f32),
                pltpu.VMEM((2 * PART // LANES * channels, LANES), f32),
                pltpu.VMEM((PARTS, n_dev, 16, PART // CHUNKS), bf16),
                pltpu.VMEM((16, WIDE), f32),
                pltpu.VMEM((2, 16, PART // CHUNKS), f32),
                pltpu.VMEM((F, LAGS), bf16),
                pltpu.VMEM((F, LAGS), bf16),
                pltpu.VMEM((total, F), bf16),
                pltpu.VMEM((total, F), bf16),
                pltpu.VMEM((16, F), f32),
                pltpu.VMEM((16, F), f32),
                pltpu.VMEM((total, LAGS), f32),
                pltpu.VMEM((groups, 8, LANES), jnp.int32),
                pltpu.VMEM((groups, 8, LANES), jnp.int32),
                pltpu.VMEM((groups, slots * 16, WIDE), bf16),
                pltpu.VMEM((groups, slots * 16, WIDE), bf16),
                pltpu.VMEM(coarse.shape, f32),
                pltpu.VMEM(fine.shape, f32),
                pltpu.SemaphoreType.DMA((4 * PARTS,)),
                pltpu.SemaphoreType.DMA((2,)),
                pltpu.SemaphoreType.DMA((n_dev * PARTS,)),
                pltpu.SemaphoreType.DMA((PARTS, n_dev)),
                pltpu.SemaphoreType.DMA((groups,)),
                pltpu.SemaphoreType.DMA((groups,)),
                pltpu.SemaphoreType.DMA((groups,)),
                pltpu.SemaphoreType.DMA((groups,)),
            ],
            compiler_params=pltpu.CompilerParams(
                collective_id=0, has_side_effects=True, vmem_limit_bytes=56 << 20
            ),
        )(source_pick, pair_remote, pair_local, spectra, jnp.asarray(coarse), jnp.asarray(fine))
        scale = 0.5 * F ** (-0.5)

        def finish(count_ref, group_ref, cross_ref, group_out, cross_out):
            group_out[...] = group_ref[...] * scale
            for h in range(groups):
                for slot in range(slots):
                    valid = slot < count_ref[0, 0, h]
                    cross_out[0, 0, h, slot:slot + 1, :] = jnp.where(valid, cross_ref[h, slot:slot + 1, :] * scale, 0.0)

        group_corr, cross_corr = pl.pallas_call(
            finish,
            out_shape=(
                jax.ShapeDtypeStruct((channels, n_dev, LAGS), f32),
                jax.ShapeDtypeStruct((1, 1, groups, slots, LAGS), f32),
            ),
            in_specs=[smem, vmem, vmem],
            out_specs=(vmem, vmem),
        )(pair_count, group_corr, cross_corr)
        return group_corr, cross_corr

    return jax.shard_map(
        on_device,
        mesh=mesh,
        in_specs=(
            P(("grp", "dev"), None, None, None),
            P(("grp", "dev")),
            P("grp", "dev", None, None),
            P("grp", "dev", None, None),
            P("grp", "dev", None),
        ),
        out_specs=(P(("grp", "dev"), None, None), P("grp", "dev", None, None, None)),
        check_vma=False,
    )
```

```python
import functools

import jax
import jax.numpy as jnp
import numpy as np
from jax import lax
from jax.experimental import pallas as pl
from jax.experimental.pallas import tpu as pltpu
from jax.sharding import PartitionSpec as P

MESH = pl.DeviceIdType.MESH
F = 4096
LAGS = 512
LAG_BLK = 128
BAND = 64
FINE = 64
CHUNKS = 4
WIDE = F // CHUNKS
LANES = 128
PARTS = 1
TABLE_CUTS = (6, 10, 14, 16)
PART = F // PARTS


def phase_tables():
    a = np.arange(F // FINE)[:, None] * np.arange(LAG_BLK)[None, :]
    coarse = np.pi * (a * FINE % (2 * F)) / F
    b = np.arange(FINE)[:, None] * (np.arange(LAGS) - LAGS // 2)[None, :]
    fine = np.pi * (b % (2 * F)) / F
    return (
        np.stack([np.cos(coarse), np.sin(coarse)]).astype(np.float32),
        np.stack([np.cos(fine), np.sin(fine)]).astype(np.float32),
    )


def kernel(
    groups, n_dev, slots, channels, pair_rows,
    pick_ref, remote_ref, local_ref, x_hbm, coarse_hbm, fine_hbm,
    group_out, cross_out,
    raw, white, mag, gathered, row_scratch, src_f32, cos_t, sin_t, xr, xi, pr, pi, acc,
    req_out, req_in, rows_out, rows_in,
    coarse_ref, fine_ref, load_sem, table_sem, send_sem, recv_sem, req_send, req_recv, row_send, row_recv,
):
    g = lax.axis_index("grp")
    d = lax.axis_index("dev")
    rows = n_dev // 4
    r, c, k = d // 4, (d // 2) % 2, d % 2
    flip_c = r * 4 + (1 - c) * 2 + k
    flip_k = r * 4 + c * 2 + (1 - k)

    def row_of(t):
        return lax.rem(r + t, rows)

    def group_of(t):
        return lax.rem(g + t, groups)

    loads = []
    for q in range(PARTS):
        cols = pl.ds(q * PART, PART)
        for sp in range(4):
            loads.append(pltpu.make_async_copy(
                x_hbm.at[:, sp // 2, sp % 2, cols], raw.at[sp, :, cols], load_sem.at[q * 4 + sp]
            ))
            loads[-1].start()
    table_loads = [
        pltpu.make_async_copy(coarse_hbm, coarse_ref, table_sem.at[0]),
        pltpu.make_async_copy(fine_hbm, fine_ref, table_sem.at[1]),
    ]
    for copy in table_loads:
        copy.start()

    barrier = pltpu.get_barrier_semaphore()
    for t in range(1, rows):
        pl.semaphore_signal(barrier, inc=1, device_id=(g, row_of(t) * 4 + c * 2 + k), device_id_type=MESH)
    pl.semaphore_signal(barrier, inc=1, device_id=(g, flip_c), device_id_type=MESH)
    pl.semaphore_signal(barrier, inc=1, device_id=(g, flip_k), device_id_type=MESH)
    for t in range(1, groups):
        pl.semaphore_signal(barrier, inc=1, device_id=(group_of(t), d), device_id_type=MESH)

    for t in range(1, groups):
        h = group_of(t)
        for slot in range(slots):
            req_out[t, slot:slot + 1, :] = jnp.full((1, LANES), remote_ref[0, 0, h, slot], jnp.int32)

    started = []

    def remote(src, dst, send, recv, target):
        return pltpu.make_async_remote_copy(
            src_ref=src, dst_ref=dst, send_sem=send, recv_sem=recv, device_id=target, device_id_type=MESH
        )

    lane_i = lax.broadcasted_iota(jnp.int32, (LANES, LANES), 0)
    lane_j = lax.broadcasted_iota(jnp.int32, (LANES, LANES), 1)
    averaging = jnp.where(lane_i // BAND == lane_j // BAND, 1.0 / BAND, 0.0).astype(jnp.bfloat16)
    width = PART // CHUNKS

    def whiten(q):
        for copy in loads[q * 4:(q + 1) * 4]:
            copy.wait()
        tiles = PART // LANES
        for s in range(2):
            for l in range(tiles):
                cols = slice(q * PART + l * LANES, q * PART + (l + 1) * LANES)
                re, im = raw[2 * s, :, cols], raw[2 * s + 1, :, cols]
                mag[(s * tiles + l) * channels:(s * tiles + l + 1) * channels, :] = jnp.sqrt(re * re + im * im)
        value = mag[...]
        high = value.astype(jnp.bfloat16)
        rest = value - high.astype(jnp.float32)
        mid = rest.astype(jnp.bfloat16)
        low = (rest - mid.astype(jnp.float32)).astype(jnp.bfloat16)
        mean = (
            jnp.dot(high, averaging, preferred_element_type=jnp.float32)
            + jnp.dot(mid, averaging, preferred_element_type=jnp.float32)
            + jnp.dot(low, averaging, preferred_element_type=jnp.float32)
        )
        mag[...] = 1.0 / (mean + 1e-05)
        for s in range(2):
            for l in range(tiles):
                cols = slice(q * PART + l * LANES, q * PART + (l + 1) * LANES)
                inverse = mag[(s * tiles + l) * channels:(s * tiles + l + 1) * channels, :]
                for p in range(2):
                    scaled = raw[2 * s + p, :, cols] * inverse
                    white[2 * s + p, :, cols] = scaled.astype(jnp.bfloat16).astype(jnp.float32)

    def pick_row(channel):
        for sp in range(4):
            for i in range(CHUNKS):
                row_scratch[sp * CHUNKS + i:sp * CHUNKS + i + 1, :] = white[
                    sp, pl.ds(channel, 1), i * WIDE:(i + 1) * WIDE
                ]

    def pick_source(q):
        for sp in range(4):
            for i in range(CHUNKS):
                first = q * PART + i * width
                row_scratch[sp * CHUNKS + i:sp * CHUNKS + i + 1, :width] = white[
                    sp, pl.ds(pick_ref[0], 1), first:first + width
                ]
        gathered[q, d] = row_scratch[:, :width].astype(jnp.bfloat16)

    n_sent = [0]

    def forward(q, j, target):
        copy = remote(
            gathered.at[q, j], gathered.at[q, j], send_sem.at[n_sent[0]], recv_sem.at[q, j], (g, target)
        )
        n_sent[0] += 1
        copy.start()
        started.append(copy)

    def arrived(q, j):
        remote(gathered.at[q, j], gathered.at[q, j], send_sem.at[0], recv_sem.at[q, j], (g, flip_k)).wait_recv()

    def send_own(q):
        for t in range(1, rows):
            forward(q, d, row_of(t) * 4 + c * 2 + k)
        forward(q, d, flip_c)
        forward(q, d, flip_k)

    def pass_column(q):
        for t in range(1, rows):
            j = row_of(t) * 4 + c * 2 + k
            arrived(q, j)
            forward(q, j, flip_c)
            forward(q, j, flip_k)

    def pass_other(q):
        for t in range(rows):
            j = row_of(t) * 4 + (1 - c) * 2 + k
            arrived(q, j)
            forward(q, j, flip_k)

    coarse_rows = F // FINE

    cuts = [coarse_rows * n // 16 for n in TABLE_CUTS]

    def table_part(first, last):
        if first == last:
            return

        @pl.loop(first, last)
        def _(a):
            ac, asin = coarse_ref[0, pl.ds(a, 1), :], coarse_ref[1, pl.ds(a, 1), :]
            here = pl.ds(pl.multiple_of(a * FINE, FINE), FINE)
            for l in range(LAGS // LANES):
                cols = slice(l * LANES, (l + 1) * LANES)
                bc, bs = fine_ref[0, :, cols], fine_ref[1, :, cols]
                cos_t[here, cols] = (ac * bc - asin * bs).astype(jnp.bfloat16)
                sin_t[here, cols] = (-(asin * bc + ac * bs)).astype(jnp.bfloat16)

    whiten(0)
    pick_source(0)
    for copy in table_loads:
        copy.wait()
    table_part(0, cuts[0])
    pl.semaphore_wait(barrier, rows + 1 + groups - 1)
    send_own(0)
    for t in range(1, groups):
        copy = remote(req_out.at[t], req_in.at[g], req_send.at[t], req_recv.at[g], (group_of(t), d))
        copy.start()
        started.append(copy)
    for q in range(1, PARTS):
        whiten(q)
        pick_source(q)
        send_own(q)

    channel_id = lax.broadcasted_iota(jnp.int32, (channels, LANES), 0)
    for t in range(1, groups):
        h = group_of(t)
        remote(req_out.at[t], req_in.at[h], req_send.at[t], req_recv.at[h], (h, d)).wait_recv()
        asked = req_in[h]
        for slot in range(slots):
            chosen = channel_id == jnp.broadcast_to(asked[slot:slot + 1, :], (channels, LANES))
            chosen = jnp.concatenate([chosen] * (WIDE // LANES), axis=1)
            for sp in range(4):
                for q in range(CHUNKS):
                    part = jnp.where(chosen, white[sp, :, q * WIDE:(q + 1) * WIDE], 0.0)
                    row_scratch[sp * CHUNKS + q:sp * CHUNKS + q + 1, :] = jnp.sum(part, axis=0, keepdims=True)
            rows_out[t, slot * 16:(slot + 1) * 16, :] = row_scratch[...].astype(jnp.bfloat16)
        copy = remote(rows_out.at[t], rows_in.at[g], row_send.at[t], row_recv.at[g], (h, d))
        copy.start()
        started.append(copy)

    def cross_chip(q, first):
        for half in range(2):
            src_f32[half] = gathered[q, first + half].astype(jnp.float32)
        base = pl.multiple_of(first * channels, 2 * channels)
        for i in range(CHUNKS):
            for l in range(width // LANES):
                start = q * PART + i * width + l * LANES
                cols = slice(start, start + LANES)
                lanes = slice(l * LANES, (l + 1) * LANES)
                w = [white[sp, :, cols] for sp in range(4)]
                real, imag = [], []
                for half in range(2):
                    v = [
                        jnp.broadcast_to(
                            src_f32[half, sp * CHUNKS + i:sp * CHUNKS + i + 1, lanes], (channels, LANES)
                        )
                        for sp in range(4)
                    ]
                    real.append(w[0] * v[0] + w[1] * v[1] + w[2] * v[2] + w[3] * v[3])
                    imag.append(w[1] * v[0] - w[0] * v[1] + w[3] * v[2] - w[2] * v[3])
                xr[pl.ds(base, 2 * channels), cols] = jnp.concatenate(real, axis=0).astype(jnp.bfloat16)
                xi[pl.ds(base, 2 * channels), cols] = jnp.concatenate(imag, axis=0).astype(jnp.bfloat16)

    def cross_part(q):
        @pl.loop(0, rows)
        def _(t):
            arrived(q, row_of(t) * 4 + c * 2 + (1 - k))
            cross_chip(q, row_of(t) * 4 + c * 2)

        @pl.loop(0, rows)
        def _(t):
            arrived(q, row_of(t) * 4 + (1 - c) * 2 + (1 - k))
            cross_chip(q, row_of(t) * 4 + (1 - c) * 2)

    def multiply(q):
        here = slice(q * PART, (q + 1) * PART)
        part = jnp.dot(xr[:, here], cos_t[here, :], preferred_element_type=jnp.float32) + jnp.dot(
            xi[:, here], sin_t[here, :], preferred_element_type=jnp.float32
        )
        acc[...] = part if q == 0 else acc[...] + part

    table_part(cuts[0], cuts[1])
    pass_column(0)
    table_part(cuts[1], cuts[2])
    for q in range(1, PARTS):
        pass_column(q)
        table_part(cuts[2], cuts[3])
        pass_other(q - 1)
    if PARTS == 1:
        table_part(cuts[2], coarse_rows)
        pass_other(0)
    else:
        table_part(cuts[3], coarse_rows)

    if pair_rows:
        pr[...] = jnp.zeros_like(pr)
        pi[...] = jnp.zeros_like(pi)
    for t in range(1, groups):
        h = group_of(t)
        remote(rows_out.at[t], rows_in.at[h], row_send.at[t], row_recv.at[h], (h, d)).wait_recv()
        for slot in range(slots):
            pick_row(local_ref[0, 0, h, slot])
            there = rows_in[h, slot * 16:(slot + 1) * 16, :].astype(jnp.float32)
            here = row_scratch[...]
            w = [here[sp * CHUNKS:(sp + 1) * CHUNKS] for sp in range(4)]
            v = [there[sp * CHUNKS:(sp + 1) * CHUNKS] for sp in range(4)]
            real = w[0] * v[0] + w[1] * v[1] + w[2] * v[2] + w[3] * v[3]
            imag = w[1] * v[0] - w[0] * v[1] + w[3] * v[2] - w[2] * v[3]
            row = (t - 1) * slots + slot
            for q in range(CHUNKS):
                pr[row:row + 1, q * WIDE:(q + 1) * WIDE] = real[q:q + 1]
                pi[row:row + 1, q * WIDE:(q + 1) * WIDE] = imag[q:q + 1]
    if pair_rows:
        xr[n_dev * channels:, :] = pr[...].astype(jnp.bfloat16)
        xi[n_dev * channels:, :] = pi[...].astype(jnp.bfloat16)

    for q in range(PARTS):
        cross_part(q)
        if q + 1 < PARTS:
            pass_other(PARTS - 1)
        multiply(q)

    for j in range(n_dev):
        group_out[:, j, :] = acc[j * channels:(j + 1) * channels, :]
    cross_out[g] = jnp.zeros((slots, LAGS), jnp.float32)
    for t in range(1, groups):
        row = n_dev * channels + (t - 1) * slots
        cross_out[group_of(t)] = acc[row:row + slots, :]

    for copy in started:
        copy.wait_send()


def solution(mesh):
    groups, n_dev = mesh.shape["grp"], mesh.shape["dev"]
    coarse, fine = phase_tables()

    def on_device(spectra, source_pick, pair_remote, pair_local, pair_count):
        channels = spectra.shape[0]
        slots = pair_remote.shape[3]
        pair_rows = -(-((groups - 1) * slots) // 16) * 16
        total = n_dev * channels + pair_rows
        smem = pl.BlockSpec(memory_space=pltpu.SMEM)
        hbm = pl.BlockSpec(memory_space=pltpu.HBM)
        vmem = pl.BlockSpec(memory_space=pltpu.VMEM)
        f32, bf16 = jnp.float32, jnp.bfloat16
        group_corr, cross_corr = pl.pallas_call(
            functools.partial(kernel, groups, n_dev, slots, channels, pair_rows),
            out_shape=(
                jax.ShapeDtypeStruct((channels, n_dev, LAGS), f32),
                jax.ShapeDtypeStruct((groups, slots, LAGS), f32),
            ),
            in_specs=[smem, smem, smem, hbm, hbm, hbm],
            out_specs=(vmem, vmem),
            scratch_shapes=[
                pltpu.VMEM((4, channels, F), f32),
                pltpu.VMEM((4, channels, F), f32),
                pltpu.VMEM((2 * PART // LANES * channels, LANES), f32),
                pltpu.VMEM((PARTS, n_dev, 16, PART // CHUNKS), bf16),
                pltpu.VMEM((16, WIDE), f32),
                pltpu.VMEM((2, 16, PART // CHUNKS), f32),
                pltpu.VMEM((F, LAGS), bf16),
                pltpu.VMEM((F, LAGS), bf16),
                pltpu.VMEM((total, F), bf16),
                pltpu.VMEM((total, F), bf16),
                pltpu.VMEM((16, F), f32),
                pltpu.VMEM((16, F), f32),
                pltpu.VMEM((total, LAGS), f32),
                pltpu.VMEM((groups, 8, LANES), jnp.int32),
                pltpu.VMEM((groups, 8, LANES), jnp.int32),
                pltpu.VMEM((groups, slots * 16, WIDE), bf16),
                pltpu.VMEM((groups, slots * 16, WIDE), bf16),
                pltpu.VMEM(coarse.shape, f32),
                pltpu.VMEM(fine.shape, f32),
                pltpu.SemaphoreType.DMA((4 * PARTS,)),
                pltpu.SemaphoreType.DMA((2,)),
                pltpu.SemaphoreType.DMA((n_dev * PARTS,)),
                pltpu.SemaphoreType.DMA((PARTS, n_dev)),
                pltpu.SemaphoreType.DMA((groups,)),
                pltpu.SemaphoreType.DMA((groups,)),
                pltpu.SemaphoreType.DMA((groups,)),
                pltpu.SemaphoreType.DMA((groups,)),
            ],
            compiler_params=pltpu.CompilerParams(
                collective_id=0, has_side_effects=True, vmem_limit_bytes=56 << 20
            ),
        )(source_pick, pair_remote, pair_local, spectra, jnp.asarray(coarse), jnp.asarray(fine))
        scale = 0.5 * F ** (-0.5)

        def finish(count_ref, group_ref, cross_ref, group_out, cross_out):
            group_out[...] = group_ref[...] * scale
            for h in range(groups):
                for slot in range(slots):
                    valid = slot < count_ref[0, 0, h]
                    cross_out[0, 0, h, slot:slot + 1, :] = jnp.where(valid, cross_ref[h, slot:slot + 1, :] * scale, 0.0)

        group_corr, cross_corr = pl.pallas_call(
            finish,
            out_shape=(
                jax.ShapeDtypeStruct((channels, n_dev, LAGS), f32),
                jax.ShapeDtypeStruct((1, 1, groups, slots, LAGS), f32),
            ),
            in_specs=[smem, vmem, vmem],
            out_specs=(vmem, vmem),
        )(pair_count, group_corr, cross_corr)
        return group_corr, cross_corr

    return jax.shard_map(
        on_device,
        mesh=mesh,
        in_specs=(
            P(("grp", "dev"), None, None, None),
            P(("grp", "dev")),
            P("grp", "dev", None, None),
            P("grp", "dev", None, None),
            P("grp", "dev", None),
        ),
        out_specs=(P(("grp", "dev"), None, None), P("grp", "dev", None, None, None)),
        check_vma=False,
    )
```
